512 devices in a mesh: ctx: 32 (over y, x, z_hi), head: 16 (over z_lo, core).
Axes of the slice: x: 4, y: 4, z: 16 (z_hi: 2, z_lo: 8; z = z_hi * 8 + z_lo), core: 2. Of those that a mesh axis runs over, the one named last changes fastest.
Arguments:
- tokens: bfloat16 [14336, 5376], P('ctx'), may hold values from -6 to 6
- w_query: bfloat16 [5376, 4096], P('ctx', 'head')
- key_weight: bfloat16 [5376, 2048], P('ctx', 'head')
- value_weight: bfloat16 [5376, 2048], P('ctx', 'head'), may hold values from -0.078125 to 0.078125
- query_gain: float32 [128], replicated, may hold values from 0.5 to 16
- key_gain: float32 [128], replicated, may hold values from 0.5 to 16
Outputs:
- attended: bfloat16 [14336, 4096], P('ctx', 'head')
The draws below stay inside these ranges and needn't reach their ends.
All inputs are finite; a program needn't handle non-finite values.
Results may differ from the reference program's by a relative error of at most 0.025.
Values may be sent and summed in bfloat16 or wider, within the bound.
No kernel may reach another device: no remote copies, remote signals or barrier semaphores. Data moves between devices by JAX's collectives and lax.ppermute only.
A program may use at most 64 MiB of HBM per device.

```python
import jax
import jax.numpy as jnp
from jax import lax

MODEL_WIDTH = 5376
HEAD_WIDTH = 128
WINDOW = 1024
TOKENS_PER_SHARD = 448
KEY_VALUE_HEADS = 16
QUERY_HEADS = 32
SEQUENCE_TOKENS = 14336


def keys_shared(key):
    return jax.random.normal(jax.random.fold_in(key, 11), (MODEL_WIDTH, KEY_VALUE_HEADS * HEAD_WIDTH), jnp.float32) * MODEL_WIDTH ** (-0.5)


def draw_key_weight(key, part):
    return keys_shared(key).astype(jnp.bfloat16)


def draw_w_query(key, part):
    own = jax.random.normal(jax.random.fold_in(key, 23), (MODEL_WIDTH, QUERY_HEADS * HEAD_WIDTH), jnp.float32) * MODEL_WIDTH ** (-0.5)
    return own.astype(jnp.bfloat16)


def draw_query_gain(key, part):
    drawn = jax.random.uniform(jax.random.fold_in(key, 31), (HEAD_WIDTH,), jnp.float32, 0.5, 2.0)
    return drawn


def draw_key_gain(key, part):
    drawn = jax.random.uniform(jax.random.fold_in(key, 53), (HEAD_WIDTH,), jnp.float32, 0.5, 2.0)
    return drawn


def block_levels(stream_key, shape, cuts, least, high):
    loudness = 1.0
    for dim, shards_of in cuts:
        steps = jax.random.uniform(jax.random.fold_in(jax.random.fold_in(stream_key, 6), dim), (shards_of,), jnp.float32, least / len(cuts), high / len(cuts))
        loudness = loudness * jnp.repeat(jnp.exp(steps), shape[dim] // shards_of).reshape((-1,) + (1,) * (len(shape) - 1 - dim))
    return loudness


def noise(rng, extent, spread, most, pieces=(), kind=jnp.bfloat16):
    values = spread * jax.random.normal(rng, extent, jnp.float32)
    if pieces:
        values = values * block_levels(rng, extent, pieces, -0.22, 0.18)
    return jnp.clip(values, -most, most).astype(kind)


def setup_inputs(seed: int = 0) -> dict:
    arg_keys = jax.random.split(jax.random.key(seed), 7)
    return {
        "tokens": noise(arg_keys[0], (SEQUENCE_TOKENS, MODEL_WIDTH), 1.0, 6.0, ((0, 32),)),
        "w_query": draw_w_query(jax.random.fold_in(arg_keys[6], 71), 0),
        "key_weight": draw_key_weight(jax.random.fold_in(arg_keys[6], 71), 0),
        "value_weight": noise(arg_keys[3], (MODEL_WIDTH, KEY_VALUE_HEADS * HEAD_WIDTH), MODEL_WIDTH ** -0.5, 0.078125, ((0, 32), (1, 16))),
        "query_gain": draw_query_gain(jax.random.fold_in(arg_keys[6], 71), 0),
        "key_gain": draw_key_gain(jax.random.fold_in(arg_keys[6], 71), 0),
    }


query_scale = 168.0 ** (-0.5)

def normalize(values, gain):
    return values * lax.rsqrt(lax.optimization_barrier(jnp.mean(values * values, axis=-1, keepdims=True)) + 1e-06) * gain

def rotate(values, position):
    half = values.shape[-1] // 2
    expo = jnp.arange(half, dtype=jnp.float32) * (2.0 / values.shape[-1])
    freq = jnp.power(jnp.float32(10000.0), -expo)
    angle = position[:, None] * freq[None, :]
    cosine = jnp.cos(angle)[:, None, :]
    sine = jnp.sin(angle)[:, None, :]
    first = values[..., :half]
    second = values[..., half:]
    return jnp.concatenate([first * cosine - second * sine, second * cosine + first * sine], axis=-1)

def reference(tokens, w_query, key_weight, value_weight, query_gain, key_gain):
    position = jnp.arange(SEQUENCE_TOKENS, dtype=jnp.int32).astype(jnp.float32)
    query_sum = jnp.dot(tokens, w_query, preferred_element_type=jnp.float32).reshape(SEQUENCE_TOKENS, QUERY_HEADS, HEAD_WIDTH)
    summed_keys = jnp.dot(tokens, key_weight, preferred_element_type=jnp.float32).reshape(SEQUENCE_TOKENS, KEY_VALUE_HEADS, HEAD_WIDTH)
    summed_values = jnp.dot(tokens, value_weight, preferred_element_type=jnp.float32).reshape(SEQUENCE_TOKENS, KEY_VALUE_HEADS, HEAD_WIDTH)
    queries = rotate(normalize(query_sum, query_gain), position).astype(jnp.bfloat16)
    keys = rotate(normalize(summed_keys, key_gain), position).astype(jnp.bfloat16)
    values = summed_values.astype(jnp.bfloat16)
    reach = WINDOW - 1
    key_padded = jnp.pad(keys, ((reach, 0), (0, 0), (0, 0)))
    value_padded = jnp.pad(values, ((reach, 0), (0, 0), (0, 0)))

    def one_block(index):
        start = (index * TOKENS_PER_SHARD).astype(jnp.int32)
        query_block = lax.dynamic_slice_in_dim(queries, start, TOKENS_PER_SHARD, 0).astype(jnp.float32)
        block_k = lax.dynamic_slice_in_dim(key_padded, start, reach + TOKENS_PER_SHARD, 0).astype(jnp.float32)
        block_v = lax.dynamic_slice_in_dim(value_padded, start, reach + TOKENS_PER_SHARD, 0).astype(jnp.float32)
        query_pos = start + jnp.arange(TOKENS_PER_SHARD, dtype=jnp.int32)
        key_pos = start - reach + jnp.arange(reach + TOKENS_PER_SHARD, dtype=jnp.int32)
        allowed = (key_pos[None, :] <= query_pos[:, None]) & (key_pos[None, :] > query_pos[:, None] - WINDOW) & (key_pos[None, :] >= 0)
        grouped_heads = query_block.reshape(TOKENS_PER_SHARD, KEY_VALUE_HEADS, 2, HEAD_WIDTH)
        scores = jnp.einsum('bkgd,ckd->kgbc', grouped_heads, block_k) * query_scale
        scores = jnp.where(allowed[None, None], scores, jnp.float32(-1e+30))
        top = lax.optimization_barrier(jnp.max(scores, axis=-1, keepdims=True))
        weights = jnp.exp(scores - top)
        probs = (weights / lax.optimization_barrier(jnp.sum(weights, axis=-1, keepdims=True))).astype(jnp.bfloat16)
        mixed = jnp.einsum('kgbc,ckd->bkgd', probs.astype(jnp.float32), block_v)
        return mixed.reshape(TOKENS_PER_SHARD, QUERY_HEADS * HEAD_WIDTH).astype(jnp.bfloat16)
    blocks = lax.map(one_block, jnp.arange(SEQUENCE_TOKENS // TOKENS_PER_SHARD, dtype=jnp.int32))
    return blocks.reshape(SEQUENCE_TOKENS, QUERY_HEADS * HEAD_WIDTH)
```

```python
import jax
import jax.numpy as jnp
from jax import lax
from jax.sharding import Mesh
from jax.sharding import PartitionSpec as P

WINDOW = 1024
PLANE = ("y", "x")
CTX = ("y", "x", "zh")
HEAD = ("zl", "core")

query_scale = 168.0 ** (-0.5)


def normalize(values, gain):
    return values * lax.rsqrt(jnp.mean(values * values, axis=-1, keepdims=True) + 1e-06) * gain


def rotate(values, position):
    half = values.shape[-1] // 2
    expo = jnp.arange(half, dtype=jnp.float32) * (2.0 / values.shape[-1])
    freq = jnp.power(jnp.float32(10000.0), -expo)
    angle = position[:, None] * freq[None, :]
    cosine = jnp.cos(angle)[:, None, :]
    sine = jnp.sin(angle)[:, None, :]
    first = values[..., :half]
    second = values[..., half:]
    return jnp.concatenate(
        [first * cosine - second * sine, second * cosine + first * sine], axis=-1
    )


def from_behind(block, distance):
    count = lax.axis_size(CTX)
    return lax.ppermute(block, CTX, [(i - distance, i) for i in range(distance, count)])


def on_device(tokens, w_query, key_weight, value_weight, query_gain, key_gain):
    row_count = tokens.shape[0]
    head_size = query_gain.shape[0]
    plane = lax.axis_size(PLANE)
    q_width = w_query.shape[1]
    kv_width = 2 * head_size

    mine = jnp.concatenate([key_weight, value_weight, w_query], axis=1)
    pair = lax.all_gather(mine, "zh", axis=0, tiled=True)
    pair_kv = pair[:, :kv_width]
    pair_q = pair[:, kv_width:]
    all_q = lax.all_gather(pair_q, PLANE, axis=0, tiled=True)
    all_kv = lax.all_to_all(
        jnp.broadcast_to(pair_kv[None], (plane,) + pair_kv.shape), PLANE, 0, 0, tiled=True
    ).reshape(-1, kv_width)

    offset = lax.axis_index(CTX) * row_count
    local_pos = offset + jnp.arange(row_count, dtype=jnp.int32)
    position = local_pos.astype(jnp.float32)

    kv_sum = jnp.dot(tokens, all_kv, preferred_element_type=jnp.float32)
    keys = rotate(normalize(kv_sum[:, None, :head_size], key_gain), position)[:, 0]
    kv = jnp.concatenate(
        [keys.astype(jnp.bfloat16), kv_sum[:, head_size:].astype(jnp.bfloat16)], axis=1
    )
    reach = WINDOW - 1
    hop_count = (reach + row_count - 1) // row_count
    needed = [min(row_count, reach - distance * row_count) for distance in range(hop_count)]
    sizes = [-(-rows // 16) * 16 for rows in needed]
    received = [
        from_behind(kv[row_count - size :], distance + 1) for distance, size in enumerate(sizes)
    ]
    before = sum(sizes)
    all_keys_values = jnp.concatenate(received[::-1] + [kv], axis=0)
    key_pos = offset - before + jnp.arange(before + row_count, dtype=jnp.int32)

    query_sum = jnp.dot(tokens, all_q, preferred_element_type=jnp.float32)
    queries = rotate(
        normalize(query_sum.reshape(row_count, 2, head_size), query_gain), position
    ).astype(jnp.bfloat16)

    allowed = (
        (key_pos[None, :] <= local_pos[:, None])
        & (key_pos[None, :] > local_pos[:, None] - WINDOW)
        & (key_pos[None, :] >= 0)
    )
    scores = (
        jnp.einsum(
            "bgd,cd->gbc",
            queries,
            all_keys_values[:, :head_size],
            preferred_element_type=jnp.float32,
        )
        * query_scale
    )
    scores = jnp.where(allowed[None], scores, jnp.float32(-1e30))
    top = jnp.max(scores, axis=-1, keepdims=True)
    weights = jnp.exp(scores - top)
    probs = (weights / jnp.sum(weights, axis=-1, keepdims=True)).astype(jnp.bfloat16)
    mixed = jnp.einsum(
        "gbc,cd->bgd", probs, all_keys_values[:, head_size:], preferred_element_type=jnp.float32
    )
    return mixed.reshape(row_count, q_width).astype(jnp.bfloat16)


def solution(mesh):
    split = Mesh(mesh.devices.reshape(4, 4, 2, 8, 2), CTX + HEAD)
    placed = (P(CTX, None), P(CTX, HEAD), P(CTX, HEAD), P(CTX, HEAD), P(), P())
    return jax.shard_map(
        on_device, mesh=split, in_specs=placed, out_specs=P(CTX, HEAD), check_vma=False
    )
```

```python
import itertools

import jax
import jax.numpy as jnp
from jax import lax
from jax.experimental import pallas as pl
from jax.experimental.pallas import tpu as pltpu
from jax.sharding import Mesh
from jax.sharding import PartitionSpec as P

WINDOW = 1024
SIDE = 4
CTX = ("y", "x", "zh")
HEAD = ("zl", "core")
QUERY_BLOCK = 64

query_scale = 168.0 ** (-0.5)


def rings(stage):
    groups = []
    for zh, zl, core in itertools.product(range(2), range(8), range(2)):
        for fixed in range(SIDE):
            places = [(fixed, i) if core == stage else (i, fixed) for i in range(SIDE)]
            groups.append([(((y * SIDE + x) * 2 + zh) * 8 + zl) * 2 + core for y, x in places])
    return groups


def round_ring(block, stage):
    sent = jnp.broadcast_to(block[None], (SIDE,) + block.shape)
    return lax.all_to_all(sent, CTX + HEAD, 0, 0, tiled=True, axis_index_groups=rings(stage))


def from_behind(block, distance):
    count = lax.axis_size(CTX)
    return lax.ppermute(block, CTX, [(i - distance, i) for i in range(distance, count)])


def rotary_tables(position, head_size):
    half = head_size // 2
    expo = jnp.arange(half, dtype=jnp.float32) * (2.0 / head_size)
    freq = jnp.power(jnp.float32(10000.0), -expo)
    angle = position[:, None] * freq[None, :]
    cosine = jnp.cos(angle)
    sine = jnp.sin(angle)
    return jnp.concatenate([cosine, cosine], 1), jnp.concatenate([-sine, sine], 1)


def projection(tokens, weight, gain, cosine, sine, core, normed_heads):
    row_count, width = tokens.shape
    columns = weight.shape[-1]
    head_size = gain.shape[-1]
    block = weight.shape[-2]
    weight = weight.reshape(SIDE * SIDE, block, columns)

    def body(core_ref, tokens_ref, weight_ref, gain_ref, cosine_ref, sine_ref, out_ref, rows_ref):
        first = core_ref[0] == 0
        for y, x in itertools.product(range(SIDE), range(SIDE)):
            place = y * SIDE + x
            source = jnp.where(first, place, x * SIDE + y)
            rows_ref[place * block : (place + 1) * block, :] = weight_ref[source]
        total = jnp.dot(tokens_ref[...], rows_ref[...], preferred_element_type=jnp.float32)
        for head in range(columns // head_size):
            span = slice(head * head_size, (head + 1) * head_size)
            values = total[:, span]
            if head < normed_heads:
                mean = jnp.mean(values * values, axis=-1, keepdims=True)
                values = values * lax.rsqrt(mean + 1e-06) * gain_ref[...]
                turned = pltpu.roll(values, head_size // 2, 1)
                values = values * cosine_ref[...] + turned * sine_ref[...]
            out_ref[:, span] = values.astype(out_ref.dtype)

    whole = pl.BlockSpec(memory_space=pltpu.VMEM)
    return pl.pallas_call(
        body,
        out_shape=jax.ShapeDtypeStruct((row_count, columns), jnp.bfloat16),
        in_specs=[pl.BlockSpec(memory_space=pltpu.SMEM)] + [whole] * 5,
        out_specs=whole,
        scratch_shapes=[pltpu.VMEM((width, columns), jnp.bfloat16)],
        compiler_params=pltpu.CompilerParams(vmem_limit_bytes=40 << 20),
        cost_estimate=pl.CostEstimate(
            flops=2 * row_count * width * columns,
            transcendentals=0,
            bytes_accessed=2 * width * (row_count + columns),
        ),
        name="projection",
    )(core, tokens, weight, gain.reshape(1, -1), cosine, sine)


def attention(queries, pieces, offset):
    row_count, q_width = queries.shape
    head_size = pieces[0].shape[1] // 2
    heads = q_width // head_size
    sizes = [piece.shape[0] for piece in pieces]
    before = sum(sizes[:-1])
    reach = before + QUERY_BLOCK

    def body(offset_ref, queries_ref, *refs):
        piece_refs, out_ref, all_ref = refs[:-2], refs[-2], refs[-1]
        start = 0
        for piece_ref, size in zip(piece_refs, sizes):
            all_ref[start : start + size, :] = piece_ref[...]
            start += size
        shape = (heads, QUERY_BLOCK, reach)
        row = lax.broadcasted_iota(jnp.int32, shape, 1).reshape(heads * QUERY_BLOCK, reach)
        column = lax.broadcasted_iota(jnp.int32, shape, 2).reshape(heads * QUERY_BLOCK, reach)
        lag = row + before - column
        in_window = (lag >= 0) & (lag < WINDOW)
        for first in range(0, row_count, QUERY_BLOCK):
            rows = slice(first, first + QUERY_BLOCK)
            keys = all_ref[first : first + reach, :head_size]
            values = all_ref[first : first + reach, head_size:]
            block = jnp.concatenate(
                [
                    queries_ref[rows, head * head_size : (head + 1) * head_size]
                    for head in range(heads)
                ],
                axis=0,
            )
            scores = lax.dot_general(
                block, keys, (((1,), (1,)), ((), ())), preferred_element_type=jnp.float32
            )
            allowed = in_window & (column >= before - first - offset_ref[0])
            scores = jnp.where(allowed, scores * query_scale, jnp.float32(-1e30))
            top = jnp.max(scores, axis=-1, keepdims=True)
            weights = jnp.exp(scores - top)
            total = jnp.sum(weights, axis=-1, keepdims=True)
            mixed = jnp.dot(
                weights.astype(jnp.bfloat16), values, preferred_element_type=jnp.float32
            )
            mixed = mixed / total
            for head in range(heads):
                out_ref[rows, head * head_size : (head + 1) * head_size] = mixed[
                    head * QUERY_BLOCK : (head + 1) * QUERY_BLOCK
                ].astype(out_ref.dtype)

    whole = pl.BlockSpec(memory_space=pltpu.VMEM)
    return pl.pallas_call(
        body,
        out_shape=jax.ShapeDtypeStruct((row_count, q_width), jnp.bfloat16),
        in_specs=[pl.BlockSpec(memory_space=pltpu.SMEM)] + [whole] * (1 + len(pieces)),
        out_specs=whole,
        scratch_shapes=[pltpu.VMEM((before + row_count, 2 * head_size), jnp.bfloat16)],
        compiler_params=pltpu.CompilerParams(vmem_limit_bytes=32 << 20),
        cost_estimate=pl.CostEstimate(
            flops=4 * row_count * q_width * reach,
            transcendentals=row_count * heads * reach,
            bytes_accessed=4 * (row_count * q_width + (before + row_count) * head_size),
        ),
        name="attention",
    )(offset.reshape(1), queries, *pieces)


def on_device(tokens, w_query, key_weight, value_weight, query_gain, key_gain):
    row_count = tokens.shape[0]
    head_size = query_gain.shape[0]
    kv_width = 2 * head_size
    low = lax.axis_index("zh") == 0
    core = lax.axis_index("core").astype(jnp.int32).reshape(1)

    mine = jnp.concatenate([key_weight, value_weight, w_query], axis=1)
    other = lax.ppermute(mine, "zh", [(0, 1), (1, 0)])
    pair = jnp.where(
        low, jnp.concatenate([mine, other], axis=0), jnp.concatenate([other, mine], axis=0)
    )
    line = round_ring(pair, 0)
    all_kv = round_ring(line[:, :, :kv_width], 1)
    line_q, all_kv = lax.optimization_barrier((line[:, :, kv_width:], all_kv))
    all_q = round_ring(line_q, 1)

    offset = (lax.axis_index(CTX) * row_count).astype(jnp.int32)
    position = (offset + jnp.arange(row_count, dtype=jnp.int32)).astype(jnp.float32)
    cosine, sine = rotary_tables(position, head_size)

    kv = projection(tokens, all_kv, key_gain, cosine, sine, core, 1)
    reach = WINDOW - 1
    hop_count = (reach + row_count - 1) // row_count
    needed = [min(row_count, reach - distance * row_count) for distance in range(hop_count)]
    sizes = [-(-rows // 16) * 16 for rows in needed]
    received = [
        from_behind(kv[row_count - size :], distance + 1) for distance, size in enumerate(sizes)
    ]
    queries = projection(tokens, all_q, query_gain, cosine, sine, core, 2)
    return attention(queries, received[::-1] + [kv], offset)


def solution(mesh):
    split = Mesh(mesh.devices.reshape(SIDE, SIDE, 2, 8, 2), CTX + HEAD)
    placed = (P(CTX, None), P(CTX, HEAD), P(CTX, HEAD), P(CTX, HEAD), P(), P())
    return jax.shard_map(
        on_device, mesh=split, in_specs=placed, out_specs=P(CTX, HEAD), check_vma=False
    )
```

```python
import itertools

import jax
import jax.numpy as jnp
from jax import lax
from jax.experimental import pallas as pl
from jax.experimental.pallas import tpu as pltpu
from jax.sharding import Mesh
from jax.sharding import PartitionSpec as P

WINDOW = 1024
SIDE = 4
SHIFTS = (0, 1, 3, 2)
CTX = ("y", "x", "zh")
HEAD = ("zl", "core")
QUERY_BLOCK = 64
COST = 10**10

query_scale = 168.0 ** (-0.5)


def rings(stage):
    groups = []
    for zh, zl, core in itertools.product(range(2), range(8), range(2)):
        for fixed in range(SIDE):
            places = [(fixed, i) if core == stage else (i, fixed) for i in range(SIDE)]
            groups.append([(((y * SIDE + x) * 2 + zh) * 8 + zl) * 2 + core for y, x in places])
    return groups


def round_ring(block, stage):
    sent = jnp.broadcast_to(block[None], (SIDE,) + block.shape)
    return lax.all_to_all(sent, CTX + HEAD, 0, 0, tiled=True, axis_index_groups=rings(stage))


def along_ring(block, stage, distance):
    pairs = [(ring[i - distance], ring[i]) for ring in rings(stage) for i in range(SIDE)]
    return lax.ppermute(block, CTX + HEAD, pairs)


def from_behind(block, distance):
    count = lax.axis_size(CTX)
    return lax.ppermute(block, CTX, [(i - distance, i) for i in range(distance, count)])


def rotary_tables(position, head_size):
    half = head_size // 2
    expo = jnp.arange(half, dtype=jnp.float32) * (2.0 / head_size)
    freq = jnp.power(jnp.float32(10000.0), -expo)
    angle = position[:, None] * freq[None, :]
    cosine = jnp.cos(angle)
    sine = jnp.sin(angle)
    return jnp.stack(
        [jnp.concatenate([cosine, cosine], 1), jnp.concatenate([-sine, sine], 1)]
    )


def projection(tokens, weight, order, gain, tables, normed_heads, tail=0):
    row_count, width = tokens.shape
    columns = weight.shape[-1]
    head_size = gain.shape[-1]
    block = weight.shape[-2]
    weight = weight.reshape(SIDE * SIDE, block, columns)

    tables = pltpu.with_memory_space_constraint(tables, pltpu.HBM)

    def body(order_ref, tokens_ref, weight_ref, gain_ref, tables_ref, *refs):
        out_refs = refs[:-3]
        out_ref = out_refs[0]
        here_ref, rows_ref, sem = refs[-3:]
        copy = pltpu.make_async_copy(tables_ref, here_ref, sem)
        copy.start()
        for place in range(SIDE * SIDE):
            rows_ref[place * block : (place + 1) * block, :] = weight_ref[order_ref[place]]
        total = jnp.dot(tokens_ref[...], rows_ref[...], preferred_element_type=jnp.float32)
        copy.wait()
        for head in range(columns // head_size):
            span = slice(head * head_size, (head + 1) * head_size)
            values = total[:, span]
            if head < normed_heads:
                mean = jnp.mean(values * values, axis=-1, keepdims=True)
                values = values * lax.rsqrt(mean + 1e-06) * gain_ref[...]
                turned = pltpu.roll(values, head_size // 2, 1)
                values = values * here_ref[0] + turned * here_ref[1]
            out_ref[:, span] = values.astype(out_ref.dtype)
        if tail:
            out_refs[1][...] = out_ref[row_count - tail :, :]

    sizes = [row_count] + [tail] * bool(tail)
    whole = pl.BlockSpec(memory_space=pltpu.VMEM)
    return pl.pallas_call(
        body,
        out_shape=[jax.ShapeDtypeStruct((size, columns), jnp.bfloat16) for size in sizes],
        in_specs=[pl.BlockSpec(memory_space=pltpu.SMEM)]
        + [whole] * 3
        + [pl.BlockSpec(memory_space=pltpu.HBM)],
        out_specs=[whole] * len(sizes),
        scratch_shapes=[
            pltpu.VMEM(tables.shape, tables.dtype),
            pltpu.VMEM((width, columns), jnp.bfloat16),
            pltpu.SemaphoreType.DMA,
        ],
        compiler_params=pltpu.CompilerParams(vmem_limit_bytes=12 << 20),
        cost_estimate=pl.CostEstimate(flops=0, transcendentals=0, bytes_accessed=0),
        name="projection",
    )(order, tokens, weight, gain.reshape(1, -1), tables)


def passed_on(rows):
    def body(rows_ref, out_ref):
        out_ref[...] = rows_ref[...]

    whole = pl.BlockSpec(memory_space=pltpu.VMEM)
    return pl.pallas_call(
        body,
        out_shape=jax.ShapeDtypeStruct(rows.shape, rows.dtype),
        in_specs=[whole],
        out_specs=whole,
        cost_estimate=pl.CostEstimate(flops=COST, transcendentals=0, bytes_accessed=rows.size * 4),
        name="passed_on",
    )(rows)


def attention(queries, pieces, offset):
    row_count, q_width = queries.shape
    head_size = pieces[0].shape[1] // 2
    heads = q_width // head_size
    sizes = [piece.shape[0] for piece in pieces]
    before = sum(sizes[:-1])
    reach = before + QUERY_BLOCK

    def body(offset_ref, queries_ref, *refs):
        piece_refs, out_ref, all_ref = refs[:-2], refs[-2], refs[-1]
        start = 0
        for piece_ref, size in zip(piece_refs, sizes):
            all_ref[start : start + size, :] = piece_ref[...]
            start += size
        shape = (heads, QUERY_BLOCK, reach)
        row = lax.broadcasted_iota(jnp.int32, shape, 1).reshape(heads * QUERY_BLOCK, reach)
        column = lax.broadcasted_iota(jnp.int32, shape, 2).reshape(heads * QUERY_BLOCK, reach)
        lag = row + before - column
        in_window = (lag >= 0) & (lag < WINDOW)
        for first in range(0, row_count, QUERY_BLOCK):
            rows = slice(first, first + QUERY_BLOCK)
            keys = all_ref[first : first + reach, :head_size]
            values = all_ref[first : first + reach, head_size:]
            block = jnp.concatenate(
                [
                    queries_ref[rows, head * head_size : (head + 1) * head_size]
                    for head in range(heads)
                ],
                axis=0,
            )
            scores = lax.dot_general(
                block, keys, (((1,), (1,)), ((), ())), preferred_element_type=jnp.float32
            )
            allowed = in_window & (column >= before - first - offset_ref[0])
            scores = jnp.where(allowed, scores * query_scale, jnp.float32(-1e30))
            top = jnp.max(scores, axis=-1, keepdims=True)
            weights = jnp.exp(scores - top)
            total = jnp.sum(weights, axis=-1, keepdims=True)
            mixed = jnp.dot(
                weights.astype(jnp.bfloat16), values, preferred_element_type=jnp.float32
            )
            mixed = mixed / total
            for head in range(heads):
                out_ref[rows, head * head_size : (head + 1) * head_size] = mixed[
                    head * QUERY_BLOCK : (head + 1) * QUERY_BLOCK
                ].astype(out_ref.dtype)

    whole = pl.BlockSpec(memory_space=pltpu.VMEM)
    return pl.pallas_call(
        body,
        out_shape=jax.ShapeDtypeStruct((row_count, q_width), jnp.bfloat16),
        in_specs=[pl.BlockSpec(memory_space=pltpu.SMEM)] + [whole] * (1 + len(pieces)),
        out_specs=whole,
        scratch_shapes=[pltpu.VMEM((before + row_count, 2 * head_size), jnp.bfloat16)],
        compiler_params=pltpu.CompilerParams(vmem_limit_bytes=12 << 20),
        cost_estimate=pl.CostEstimate(
            flops=4 * row_count * q_width * reach,
            transcendentals=row_count * heads * reach,
            bytes_accessed=4 * (row_count * q_width + (before + row_count) * head_size),
        ),
        name="attention",
    )(offset.reshape(1), queries, *pieces)


def on_device(tokens, w_query, key_weight, value_weight, query_gain, key_gain):
    row_count = tokens.shape[0]
    head_size = query_gain.shape[0]
    kv_width = 2 * head_size
    low = lax.axis_index("zh") == 0

    mine = jnp.concatenate([key_weight, value_weight, w_query], axis=1)
    other = lax.ppermute(mine, "zh", [(0, 1), (1, 0)])
    pair = jnp.where(
        low, jnp.concatenate([mine, other], axis=0), jnp.concatenate([other, mine], axis=0)
    )
    line = round_ring(pair, 0)
    all_kv = round_ring(line[:, :, :kv_width], 1)

    offset = (lax.axis_index(CTX) * row_count).astype(jnp.int32)
    position = (offset + jnp.arange(row_count, dtype=jnp.int32)).astype(jnp.float32)
    tables = rotary_tables(position, head_size)

    all_kv, tables = lax.optimization_barrier((all_kv, tables))
    line_q = line[:, :, kv_width:]
    all_q = jnp.stack([line_q] + [along_ring(line_q, 1, shift) for shift in SHIFTS[1:]])

    y = jnp.repeat(jnp.arange(SIDE, dtype=jnp.int32), SIDE)
    x = jnp.tile(jnp.arange(SIDE, dtype=jnp.int32), SIDE)
    first_core = lax.axis_index("core") == 0
    outer = jnp.where(first_core, y, x)
    inner = jnp.where(first_core, x, y)
    here = jnp.where(first_core, lax.axis_index("y"), lax.axis_index("x"))
    shift = (here - outer) % SIDE
    kv_order = outer * SIDE + inner
    q_order = jnp.where(shift == 2, 3, jnp.where(shift == 3, 2, shift)) * SIDE + inner

    far_rows = -(-(WINDOW - 1 - 2 * row_count) // 16) * 16
    kv, tail = projection(tokens, all_kv, kv_order, key_gain, tables, 1, far_rows)
    near = from_behind(kv, 1)
    far = from_behind(tail, 3)
    middle = from_behind(passed_on(kv), 2)
    (queries,) = projection(tokens, all_q, q_order, query_gain, tables, 2)
    return attention(queries, [far, middle, near, kv], offset)


def solution(mesh):
    split = Mesh(mesh.devices.reshape(SIDE, SIDE, 2, 8, 2), CTX + HEAD)
    placed = (P(CTX, None), P(CTX, HEAD), P(CTX, HEAD), P(CTX, HEAD), P(), P())
    return jax.shard_map(
        on_device, mesh=split, in_specs=placed, out_specs=P(CTX, HEAD), check_vma=False
    )
```

```python
import itertools

import jax
import jax.numpy as jnp
from jax import lax
from jax.experimental import pallas as pl
from jax.experimental.pallas import tpu as pltpu
from jax.sharding import Mesh
from jax.sharding import PartitionSpec as P

WINDOW = 1024
SIDE = 4
SHIFTS = (0, 1, 3, 2)
CTX = ("y", "x", "zh")
HEAD = ("zl", "core")
QUERY_BLOCK = 64
OPERANDS = (0, 2, 1, 3)

query_scale = 168.0 ** (-0.5)


def rings(stage):
    groups = []
    for zh, zl, core in itertools.product(range(2), range(8), range(2)):
        for fixed in range(SIDE):
            places = [(fixed, i) if core == stage else (i, fixed) for i in range(SIDE)]
            groups.append([(((y * SIDE + x) * 2 + zh) * 8 + zl) * 2 + core for y, x in places])
    return groups


def round_ring(block, stage):
    sent = jnp.broadcast_to(block[None], (SIDE,) + block.shape)
    return lax.all_to_all(sent, CTX + HEAD, 0, 0, tiled=True, axis_index_groups=rings(stage))


def along_ring(block, stage, distance):
    pairs = [(ring[i - distance], ring[i]) for ring in rings(stage) for i in range(SIDE)]
    return lax.ppermute(block, CTX + HEAD, pairs)


def from_behind(block, distance):
    count = lax.axis_size(CTX)
    return lax.ppermute(block, CTX, [(i - distance, i) for i in range(distance, count)])


def rotary_tables(position, head_size):
    half = head_size // 2
    expo = jnp.arange(half, dtype=jnp.float32) * (2.0 / head_size)
    freq = jnp.power(jnp.float32(10000.0), -expo)
    angle = position[:, None] * freq[None, :]
    cosine = jnp.cos(angle)
    sine = jnp.sin(angle)
    return jnp.stack(
        [jnp.concatenate([cosine, cosine], 1), jnp.concatenate([-sine, sine], 1)]
    )


def side_by_side(*arrays):
    widths = [array.shape[1] for array in arrays]

    def body(*refs):
        start = 0
        for ref, width in zip(refs, widths):
            refs[-1][:, start : start + width] = ref[...]
            start += width

    whole = pl.BlockSpec(memory_space=pltpu.VMEM)
    return pl.pallas_call(
        body,
        out_shape=jax.ShapeDtypeStruct((arrays[0].shape[0], sum(widths)), arrays[0].dtype),
        in_specs=[whole] * len(arrays),
        out_specs=whole,
        name="side_by_side",
    )(*arrays)


def projection(tokens, weight, order, gain, tables, normed_heads, tail=0):
    row_count, width = tokens.shape
    columns = weight.shape[-1]
    head_size = gain.shape[-1]
    block = weight.shape[-2]
    weight = weight.reshape(SIDE * SIDE, block, columns)

    tables = pltpu.with_memory_space_constraint(tables, pltpu.HBM)

    def body(order_ref, tokens_ref, weight_ref, gain_ref, tables_ref, *refs):
        out_refs = refs[:-3]
        out_ref = out_refs[0]
        here_ref, rows_ref, sem = refs[-3:]
        copy = pltpu.make_async_copy(tables_ref, here_ref, sem)
        copy.start()
        for place in range(SIDE * SIDE):
            rows_ref[place * block : (place + 1) * block, :] = weight_ref[order_ref[place]]
        total = jnp.dot(tokens_ref[...], rows_ref[...], preferred_element_type=jnp.float32)
        copy.wait()
        for head in range(columns // head_size):
            span = slice(head * head_size, (head + 1) * head_size)
            values = total[:, span]
            if head < normed_heads:
                mean = jnp.mean(values * values, axis=-1, keepdims=True)
                values = values * lax.rsqrt(mean + 1e-06) * gain_ref[...]
                turned = pltpu.roll(values, head_size // 2, 1)
                values = values * here_ref[0] + turned * here_ref[1]
            out_ref[:, span] = values.astype(out_ref.dtype)
        if tail:
            out_refs[1][...] = out_ref[row_count - tail :, :]

    sizes = [row_count] + [tail] * bool(tail)
    whole = pl.BlockSpec(memory_space=pltpu.VMEM)
    return pl.pallas_call(
        body,
        out_shape=[jax.ShapeDtypeStruct((size, columns), jnp.bfloat16) for size in sizes],
        in_specs=[pl.BlockSpec(memory_space=pltpu.SMEM)]
        + [whole] * 3
        + [pl.BlockSpec(memory_space=pltpu.HBM)],
        out_specs=[whole] * len(sizes),
        scratch_shapes=[
            pltpu.VMEM(tables.shape, tables.dtype),
            pltpu.VMEM((width, columns), jnp.bfloat16),
            pltpu.SemaphoreType.DMA,
        ],
        compiler_params=pltpu.CompilerParams(vmem_limit_bytes=12 << 20),
        cost_estimate=pl.CostEstimate(flops=0, transcendentals=0, bytes_accessed=0),
        name="projection",
    )(order, tokens, weight, gain.reshape(1, -1), tables)


def attention(queries, pieces, offset):
    row_count, q_width = queries.shape
    head_size = pieces[0].shape[1] // 2
    heads = q_width // head_size
    sizes = [piece.shape[0] for piece in pieces]
    before = sum(sizes[:-1])
    starts = [sum(sizes[:i]) for i in range(len(sizes))]
    reach = before + QUERY_BLOCK

    def body(offset_ref, queries_ref, *refs):
        piece_refs, out_ref, all_ref = refs[:-2], refs[-2], refs[-1]
        for piece_ref, i in zip(piece_refs, OPERANDS):
            all_ref[starts[i] : starts[i] + sizes[i], :] = piece_ref[...]
        shape = (heads, QUERY_BLOCK, reach)
        row = lax.broadcasted_iota(jnp.int32, shape, 1).reshape(heads * QUERY_BLOCK, reach)
        column = lax.broadcasted_iota(jnp.int32, shape, 2).reshape(heads * QUERY_BLOCK, reach)
        lag = row + before - column
        in_window = (lag >= 0) & (lag < WINDOW)
        for first in range(0, row_count, QUERY_BLOCK):
            rows = slice(first, first + QUERY_BLOCK)
            keys = all_ref[first : first + reach, :head_size]
            values = all_ref[first : first + reach, head_size:]
            block = jnp.concatenate(
                [
                    queries_ref[rows, head * head_size : (head + 1) * head_size]
                    for head in range(heads)
                ],
                axis=0,
            )
            scores = lax.dot_general(
                block, keys, (((1,), (1,)), ((), ())), preferred_element_type=jnp.float32
            )
            allowed = in_window & (column >= before - first - offset_ref[0])
            scores = jnp.where(allowed, scores * query_scale, jnp.float32(-1e30))
            top = jnp.max(scores, axis=-1, keepdims=True)
            weights = jnp.exp(scores - top)
            total = jnp.sum(weights, axis=-1, keepdims=True)
            mixed = jnp.dot(
                weights.astype(jnp.bfloat16), values, preferred_element_type=jnp.float32
            )
            mixed = mixed / total
            for head in range(heads):
                out_ref[rows, head * head_size : (head + 1) * head_size] = mixed[
                    head * QUERY_BLOCK : (head + 1) * QUERY_BLOCK
                ].astype(out_ref.dtype)

    whole = pl.BlockSpec(memory_space=pltpu.VMEM)
    return pl.pallas_call(
        body,
        out_shape=jax.ShapeDtypeStruct((row_count, q_width), jnp.bfloat16),
        in_specs=[pl.BlockSpec(memory_space=pltpu.SMEM)] + [whole] * (1 + len(pieces)),
        out_specs=whole,
        scratch_shapes=[pltpu.VMEM((before + row_count, 2 * head_size), jnp.bfloat16)],
        compiler_params=pltpu.CompilerParams(vmem_limit_bytes=12 << 20),
        cost_estimate=pl.CostEstimate(
            flops=4 * row_count * q_width * reach,
            transcendentals=row_count * heads * reach,
            bytes_accessed=4 * (row_count * q_width + (before + row_count) * head_size),
        ),
        name="attention",
    )(offset.reshape(1), queries, *[pieces[i] for i in OPERANDS])


def on_device(tokens, w_query, key_weight, value_weight, query_gain, key_gain):
    row_count = tokens.shape[0]
    head_size = query_gain.shape[0]
    kv_width = 2 * head_size
    low = lax.axis_index("zh") == 0

    mine = side_by_side(key_weight, value_weight, w_query)
    other = lax.ppermute(mine, "zh", [(0, 1), (1, 0)])
    pair = jnp.where(
        low, jnp.concatenate([mine, other], axis=0), jnp.concatenate([other, mine], axis=0)
    )
    line = round_ring(pair, 0)
    all_kv = round_ring(line[:, :, :kv_width], 1)

    offset = (lax.axis_index(CTX) * row_count).astype(jnp.int32)
    position = (offset + jnp.arange(row_count, dtype=jnp.int32)).astype(jnp.float32)
    tables = rotary_tables(position, head_size)

    all_kv, tables = lax.optimization_barrier((all_kv, tables))
    line_q = line[:, :, kv_width:]
    all_q = jnp.stack([line_q] + [along_ring(line_q, 1, shift) for shift in SHIFTS[1:]])

    y = jnp.repeat(jnp.arange(SIDE, dtype=jnp.int32), SIDE)
    x = jnp.tile(jnp.arange(SIDE, dtype=jnp.int32), SIDE)
    first_core = lax.axis_index("core") == 0
    outer = jnp.where(first_core, y, x)
    inner = jnp.where(first_core, x, y)
    here = jnp.where(first_core, lax.axis_index("y"), lax.axis_index("x"))
    shift = (here - outer) % SIDE
    kv_order = outer * SIDE + inner
    q_order = jnp.where(shift == 2, 3, jnp.where(shift == 3, 2, shift)) * SIDE + inner

    far_rows = -(-(WINDOW - 1 - 2 * row_count) // 16) * 16
    kv, tail = projection(tokens, all_kv, kv_order, key_gain, tables, 1, far_rows)
    near = from_behind(kv, 1)
    far = from_behind(tail, 3)
    middle = from_behind(kv, 2)
    (queries,) = projection(tokens, all_q, q_order, query_gain, tables, 2)
    return attention(queries, [far, middle, near, kv], offset)


def solution(mesh):
    split = Mesh(mesh.devices.reshape(SIDE, SIDE, 2, 8, 2), CTX + HEAD)
    placed = (P(CTX, None), P(CTX, HEAD), P(CTX, HEAD), P(CTX, HEAD), P(), P())
    return jax.shard_map(
        on_device, mesh=split, in_specs=placed, out_specs=P(CTX, HEAD), check_vma=False
    )
```

```python
import itertools

import jax
import jax.numpy as jnp
from jax import lax
from jax.experimental import pallas as pl
from jax.experimental.pallas import tpu as pltpu
from jax.sharding import Mesh
from jax.sharding import PartitionSpec as P

WINDOW = 1024
SIDE = 4
SHIFTS = (0, 1, 3, 2)
CTX = ("y", "x", "zh")
HEAD = ("zl", "core")
QUERY_BLOCK = 64
OPERANDS = (0, 2, 1, 3)

LOG2_E = 1.4426950408889634

query_scale = 168.0 ** (-0.5)


def rings(stage):
    groups = []
    for zh, zl, core in itertools.product(range(2), range(8), range(2)):
        for fixed in range(SIDE):
            places = [(fixed, i) if core == stage else (i, fixed) for i in range(SIDE)]
            groups.append([(((y * SIDE + x) * 2 + zh) * 8 + zl) * 2 + core for y, x in places])
    return groups


def round_ring(block, stage):
    sent = jnp.broadcast_to(block[None], (SIDE,) + block.shape)
    return lax.all_to_all(sent, CTX + HEAD, 0, 0, tiled=True, axis_index_groups=rings(stage))


def along_ring(block, stage, distance):
    pairs = [(ring[i - distance], ring[i]) for ring in rings(stage) for i in range(SIDE)]
    return lax.ppermute(block, CTX + HEAD, pairs)


def from_behind(block, distance):
    count = lax.axis_size(CTX)
    return lax.ppermute(block, CTX, [(i - distance, i) for i in range(distance, count)])


def rotary_tables(position, head_size):
    half = head_size // 2
    expo = jnp.arange(half, dtype=jnp.float32) * (2.0 / head_size)
    freq = jnp.power(jnp.float32(10000.0), -expo)
    angle = position[:, None] * freq[None, :]
    cosine = jnp.cos(angle)
    sine = jnp.sin(angle)
    return jnp.stack(
        [jnp.concatenate([cosine, cosine], 1), jnp.concatenate([-sine, sine], 1)]
    )


def side_by_side(*arrays):
    widths = [array.shape[1] for array in arrays]

    def body(*refs):
        start = 0
        for ref, width in zip(refs, widths):
            refs[-1][:, start : start + width] = ref[...]
            start += width

    whole = pl.BlockSpec(memory_space=pltpu.VMEM)
    return pl.pallas_call(
        body,
        out_shape=jax.ShapeDtypeStruct((arrays[0].shape[0], sum(widths)), arrays[0].dtype),
        in_specs=[whole] * len(arrays),
        out_specs=whole,
        name="side_by_side",
    )(*arrays)


def projection(tokens, weight, order, gain, tables, normed_heads, tail=0):
    row_count, width = tokens.shape
    columns = weight.shape[-1]
    head_size = gain.shape[-1]
    block = weight.shape[-2]
    weight = weight.reshape(SIDE * SIDE, block, columns)

    tables = pltpu.with_memory_space_constraint(tables, pltpu.HBM)

    def body(order_ref, tokens_ref, weight_ref, gain_ref, tables_ref, *refs):
        out_refs = refs[:-3]
        out_ref = out_refs[0]
        here_ref, rows_ref, sem = refs[-3:]
        copy = pltpu.make_async_copy(tables_ref, here_ref, sem)
        copy.start()
        for place in range(SIDE * SIDE):
            rows_ref[place * block : (place + 1) * block, :] = weight_ref[order_ref[place]]
        total = jnp.dot(tokens_ref[...], rows_ref[...], preferred_element_type=jnp.float32)
        copy.wait()
        for head in range(columns // head_size):
            span = slice(head * head_size, (head + 1) * head_size)
            values = total[:, span]
            if head < normed_heads:
                mean = jnp.mean(values * values, axis=-1, keepdims=True)
                values = values * lax.rsqrt(mean + 1e-06) * gain_ref[...]
                turned = pltpu.roll(values, head_size // 2, 1)
                values = values * here_ref[0] + turned * here_ref[1]
            out_ref[:, span] = values.astype(out_ref.dtype)
        if tail:
            out_refs[1][...] = out_ref[row_count - tail :, :]

    sizes = [row_count] + [tail] * bool(tail)
    whole = pl.BlockSpec(memory_space=pltpu.VMEM)
    return pl.pallas_call(
        body,
        out_shape=[jax.ShapeDtypeStruct((size, columns), jnp.bfloat16) for size in sizes],
        in_specs=[pl.BlockSpec(memory_space=pltpu.SMEM)]
        + [whole] * 3
        + [pl.BlockSpec(memory_space=pltpu.HBM)],
        out_specs=[whole] * len(sizes),
        scratch_shapes=[
            pltpu.VMEM(tables.shape, tables.dtype),
            pltpu.VMEM((width, columns), jnp.bfloat16),
            pltpu.SemaphoreType.DMA,
        ],
        compiler_params=pltpu.CompilerParams(vmem_limit_bytes=12 << 20),
        cost_estimate=pl.CostEstimate(flops=0, transcendentals=0, bytes_accessed=0),
        name="projection",
    )(order, tokens, weight, gain.reshape(1, -1), tables)


def attention(queries, pieces, offset):
    row_count, q_width = queries.shape
    head_size = pieces[0].shape[1] // 2
    heads = q_width // head_size
    sizes = [piece.shape[0] for piece in pieces]
    before = sum(sizes[:-1])
    starts = [sum(sizes[:i]) for i in range(len(sizes))]
    reach = before + QUERY_BLOCK

    def body(offset_ref, queries_ref, *refs):
        piece_refs, out_ref, all_ref = refs[:-2], refs[-2], refs[-1]
        for piece_ref, i in zip(piece_refs, OPERANDS):
            all_ref[starts[i] : starts[i] + sizes[i], :] = piece_ref[...]
        shape = (heads, QUERY_BLOCK, reach)
        row = lax.broadcasted_iota(jnp.int32, shape, 1).reshape(heads * QUERY_BLOCK, reach)
        column = lax.broadcasted_iota(jnp.int32, shape, 2).reshape(heads * QUERY_BLOCK, reach)
        lag = row + before - column
        in_window = (lag >= 0) & (lag < WINDOW)
        for first in range(0, row_count, QUERY_BLOCK):
            rows = slice(first, first + QUERY_BLOCK)
            keys = all_ref[first : first + reach, :head_size]
            values = all_ref[first : first + reach, head_size:]
            block = jnp.concatenate(
                [
                    queries_ref[rows, head * head_size : (head + 1) * head_size]
                    for head in range(heads)
                ],
                axis=0,
            )
            scores = lax.dot_general(
                block, keys, (((1,), (1,)), ((), ())), preferred_element_type=jnp.float32
            )
            allowed = in_window & (column >= before - first - offset_ref[0])
            scores = jnp.where(allowed, scores, jnp.float32(-1e30))
            top = jnp.max(scores, axis=-1, keepdims=True)
            weights = jnp.exp2((scores - top) * (query_scale * LOG2_E))
            total = jnp.sum(weights, axis=-1, keepdims=True)
            mixed = jnp.dot(
                weights.astype(jnp.bfloat16), values, preferred_element_type=jnp.float32
            )
            mixed = mixed / total
            for head in range(heads):
                out_ref[rows, head * head_size : (head + 1) * head_size] = mixed[
                    head * QUERY_BLOCK : (head + 1) * QUERY_BLOCK
                ].astype(out_ref.dtype)

    whole = pl.BlockSpec(memory_space=pltpu.VMEM)
    return pl.pallas_call(
        body,
        out_shape=jax.ShapeDtypeStruct((row_count, q_width), jnp.bfloat16),
        in_specs=[pl.BlockSpec(memory_space=pltpu.SMEM)] + [whole] * (1 + len(pieces)),
        out_specs=whole,
        scratch_shapes=[pltpu.VMEM((before + row_count, 2 * head_size), jnp.bfloat16)],
        compiler_params=pltpu.CompilerParams(vmem_limit_bytes=12 << 20),
        cost_estimate=pl.CostEstimate(
            flops=4 * row_count * q_width * reach,
            transcendentals=row_count * heads * reach,
            bytes_accessed=4 * (row_count * q_width + (before + row_count) * head_size),
        ),
        name="attention",
    )(offset.reshape(1), queries, *[pieces[i] for i in OPERANDS])


def on_device(tokens, w_query, key_weight, value_weight, query_gain, key_gain):
    row_count = tokens.shape[0]
    head_size = query_gain.shape[0]
    kv_width = 2 * head_size
    low = lax.axis_index("zh") == 0

    mine = side_by_side(key_weight, value_weight, w_query)
    other = lax.ppermute(mine, "zh", [(0, 1), (1, 0)])
    pair = jnp.where(
        low, jnp.concatenate([mine, other], axis=0), jnp.concatenate([other, mine], axis=0)
    )
    line = round_ring(pair, 0)
    all_kv = round_ring(line[:, :, :kv_width], 1)

    offset = (lax.axis_index(CTX) * row_count).astype(jnp.int32)
    position = (offset + jnp.arange(row_count, dtype=jnp.int32)).astype(jnp.float32)
    tables = rotary_tables(position, head_size)

    all_kv, tables = lax.optimization_barrier((all_kv, tables))
    line_q = line[:, :, kv_width:]
    all_q = jnp.stack([line_q] + [along_ring(line_q, 1, shift) for shift in SHIFTS[1:]])

    y = jnp.repeat(jnp.arange(SIDE, dtype=jnp.int32), SIDE)
    x = jnp.tile(jnp.arange(SIDE, dtype=jnp.int32), SIDE)
    first_core = lax.axis_index("core") == 0
    outer = jnp.where(first_core, y, x)
    inner = jnp.where(first_core, x, y)
    here = jnp.where(first_core, lax.axis_index("y"), lax.axis_index("x"))
    shift = (here - outer) % SIDE
    kv_order = outer * SIDE + inner
    q_order = jnp.where(shift == 2, 3, jnp.where(shift == 3, 2, shift)) * SIDE + inner

    far_rows = -(-(WINDOW - 1 - 2 * row_count) // 16) * 16
    kv, tail = projection(tokens, all_kv, kv_order, key_gain, tables, 1, far_rows)
    near = from_behind(kv, 1)
    far = from_behind(tail, 3)
    middle = from_behind(kv, 2)
    (queries,) = projection(tokens, all_q, q_order, query_gain, tables, 2)
    return attention(queries, [far, middle, near, kv], offset)


def solution(mesh):
    split = Mesh(mesh.devices.reshape(SIDE, SIDE, 2, 8, 2), CTX + HEAD)
    placed = (P(CTX, None), P(CTX, HEAD), P(CTX, HEAD), P(CTX, HEAD), P(), P())
    return jax.shard_map(
        on_device, mesh=split, in_specs=placed, out_specs=P(CTX, HEAD), check_vma=False
    )
```

```python
import itertools

import jax
import jax.numpy as jnp
from jax import lax
from jax.experimental import pallas as pl
from jax.experimental.pallas import tpu as pltpu
from jax.sharding import Mesh
from jax.sharding import PartitionSpec as P

WINDOW = 1024
SIDE = 4
SHIFTS = (0, 1, 3, 2)
CTX = ("y", "x", "zh")
HEAD = ("zl", "core")
QUERY_BLOCK = 112
OPERANDS = (0, 2, 1, 3)

query_scale = 168.0 ** (-0.5)


def rings(stage):
    groups = []
    for zh, zl, core in itertools.product(range(2), range(8), range(2)):
        for fixed in range(SIDE):
            places = [(fixed, i) if core == stage else (i, fixed) for i in range(SIDE)]
            groups.append([(((y * SIDE + x) * 2 + zh) * 8 + zl) * 2 + core for y, x in places])
    return groups


def round_ring(block, stage):
    sent = jnp.broadcast_to(block[None], (SIDE,) + block.shape)
    return lax.all_to_all(sent, CTX + HEAD, 0, 0, tiled=True, axis_index_groups=rings(stage))


def along_ring(block, stage, distance):
    pairs = [(ring[i - distance], ring[i]) for ring in rings(stage) for i in range(SIDE)]
    return lax.ppermute(block, CTX + HEAD, pairs)


def from_behind(block, distance):
    count = lax.axis_size(CTX)
    return lax.ppermute(block, CTX, [(i - distance, i) for i in range(distance, count)])


def rotary_tables(position, head_size):
    half = head_size // 2
    expo = jnp.arange(half, dtype=jnp.float32) * (2.0 / head_size)
    freq = jnp.power(jnp.float32(10000.0), -expo)
    angle = position[:, None] * freq[None, :]
    cosine = jnp.cos(angle)
    sine = jnp.sin(angle)
    return jnp.stack(
        [jnp.concatenate([cosine, cosine], 1), jnp.concatenate([-sine, sine], 1)]
    )


def side_by_side(*arrays):
    widths = [array.shape[1] for array in arrays]

    def body(*refs):
        start = 0
        for ref, width in zip(refs, widths):
            refs[-1][:, start : start + width] = ref[...]
            start += width

    whole = pl.BlockSpec(memory_space=pltpu.VMEM)
    return pl.pallas_call(
        body,
        out_shape=jax.ShapeDtypeStruct((arrays[0].shape[0], sum(widths)), arrays[0].dtype),
        in_specs=[whole] * len(arrays),
        out_specs=whole,
        name="side_by_side",
    )(*arrays)


def projection(tokens, weight, order, gain, tables, normed_heads, tail=0):
    row_count, width = tokens.shape
    columns = weight.shape[-1]
    head_size = gain.shape[-1]
    block = weight.shape[-2]
    weight = weight.reshape(SIDE * SIDE, block, columns)

    tables = pltpu.with_memory_space_constraint(tables, pltpu.HBM)

    def body(order_ref, tokens_ref, weight_ref, gain_ref, tables_ref, *refs):
        out_refs = refs[:-3]
        out_ref = out_refs[0]
        here_ref, rows_ref, sem = refs[-3:]
        copy = pltpu.make_async_copy(tables_ref, here_ref, sem)
        copy.start()
        for place in range(SIDE * SIDE):
            rows_ref[place * block : (place + 1) * block, :] = weight_ref[order_ref[place]]
        total = jnp.dot(tokens_ref[...], rows_ref[...], preferred_element_type=jnp.float32)
        copy.wait()
        for head in range(columns // head_size):
            span = slice(head * head_size, (head + 1) * head_size)
            values = total[:, span]
            if head < normed_heads:
                mean = jnp.mean(values * values, axis=-1, keepdims=True)
                values = values * lax.rsqrt(mean + 1e-06) * gain_ref[...]
                turned = pltpu.roll(values, head_size // 2, 1)
                values = values * here_ref[0] + turned * here_ref[1]
            out_ref[:, span] = values.astype(out_ref.dtype)
        if tail:
            out_refs[1][...] = out_ref[row_count - tail :, :]

    sizes = [row_count] + [tail] * bool(tail)
    whole = pl.BlockSpec(memory_space=pltpu.VMEM)
    return pl.pallas_call(
        body,
        out_shape=[jax.ShapeDtypeStruct((size, columns), jnp.bfloat16) for size in sizes],
        in_specs=[pl.BlockSpec(memory_space=pltpu.SMEM)]
        + [whole] * 3
        + [pl.BlockSpec(memory_space=pltpu.HBM)],
        out_specs=[whole] * len(sizes),
        scratch_shapes=[
            pltpu.VMEM(tables.shape, tables.dtype),
            pltpu.VMEM((width, columns), jnp.bfloat16),
            pltpu.SemaphoreType.DMA,
        ],
        compiler_params=pltpu.CompilerParams(vmem_limit_bytes=12 << 20),
        cost_estimate=pl.CostEstimate(flops=0, transcendentals=0, bytes_accessed=0),
        name="projection",
    )(order, tokens, weight, gain.reshape(1, -1), tables)


def attention(queries, pieces, offset):
    row_count, q_width = queries.shape
    head_size = pieces[0].shape[1] // 2
    heads = q_width // head_size
    sizes = [piece.shape[0] for piece in pieces]
    before = sum(sizes[:-1])
    starts = [sum(sizes[:i]) for i in range(len(sizes))]
    reach = before + QUERY_BLOCK

    def body(offset_ref, queries_ref, *refs):
        piece_refs, out_ref, all_ref = refs[:-2], refs[-2], refs[-1]
        for piece_ref, i in zip(piece_refs, OPERANDS):
            all_ref[starts[i] : starts[i] + sizes[i], :] = piece_ref[...]
        shape = (heads, QUERY_BLOCK, reach)
        row = lax.broadcasted_iota(jnp.int32, shape, 1).reshape(heads * QUERY_BLOCK, reach)
        column = lax.broadcasted_iota(jnp.int32, shape, 2).reshape(heads * QUERY_BLOCK, reach)
        lag = row + before - column
        in_window = (lag >= 0) & (lag < WINDOW)
        for first in range(0, row_count, QUERY_BLOCK):
            rows = slice(first, first + QUERY_BLOCK)
            keys = all_ref[first : first + reach, :head_size]
            values = all_ref[first : first + reach, head_size:]
            block = jnp.concatenate(
                [
                    queries_ref[rows, head * head_size : (head + 1) * head_size]
                    for head in range(heads)
                ],
                axis=0,
            )
            scores = lax.dot_general(
                block, keys, (((1,), (1,)), ((), ())), preferred_element_type=jnp.float32
            )
            allowed = in_window & (column >= before - first - offset_ref[0])
            scores = jnp.where(allowed, scores * query_scale, jnp.float32(-1e30))
            top = jnp.max(scores, axis=-1, keepdims=True)
            weights = jnp.exp(scores - top)
            total = jnp.sum(weights, axis=-1, keepdims=True)
            mixed = jnp.dot(
                weights.astype(jnp.bfloat16), values, preferred_element_type=jnp.float32
            )
            mixed = mixed / total
            for head in range(heads):
                out_ref[rows, head * head_size : (head + 1) * head_size] = mixed[
                    head * QUERY_BLOCK : (head + 1) * QUERY_BLOCK
                ].astype(out_ref.dtype)

    whole = pl.BlockSpec(memory_space=pltpu.VMEM)
    return pl.pallas_call(
        body,
        out_shape=jax.ShapeDtypeStruct((row_count, q_width), jnp.bfloat16),
        in_specs=[pl.BlockSpec(memory_space=pltpu.SMEM)] + [whole] * (1 + len(pieces)),
        out_specs=whole,
        scratch_shapes=[pltpu.VMEM((before + row_count, 2 * head_size), jnp.bfloat16)],
        compiler_params=pltpu.CompilerParams(vmem_limit_bytes=12 << 20),
        cost_estimate=pl.CostEstimate(
            flops=4 * row_count * q_width * reach,
            transcendentals=row_count * heads * reach,
            bytes_accessed=4 * (row_count * q_width + (before + row_count) * head_size),
        ),
        name="attention",
    )(offset.reshape(1), queries, *[pieces[i] for i in OPERANDS])


def on_device(tokens, w_query, key_weight, value_weight, query_gain, key_gain):
    row_count = tokens.shape[0]
    head_size = query_gain.shape[0]
    kv_width = 2 * head_size
    low = lax.axis_index("zh") == 0

    mine = side_by_side(key_weight, value_weight, w_query)
    other = lax.ppermute(mine, "zh", [(0, 1), (1, 0)])
    pair = jnp.where(
        low, jnp.concatenate([mine, other], axis=0), jnp.concatenate([other, mine], axis=0)
    )
    line = round_ring(pair, 0)
    all_kv = round_ring(line[:, :, :kv_width], 1)

    offset = (lax.axis_index(CTX) * row_count).astype(jnp.int32)
    position = (offset + jnp.arange(row_count, dtype=jnp.int32)).astype(jnp.float32)
    tables = rotary_tables(position, head_size)

    all_kv, tables = lax.optimization_barrier((all_kv, tables))
    line_q = line[:, :, kv_width:]
    all_q = jnp.stack([line_q] + [along_ring(line_q, 1, shift) for shift in SHIFTS[1:]])

    y = jnp.repeat(jnp.arange(SIDE, dtype=jnp.int32), SIDE)
    x = jnp.tile(jnp.arange(SIDE, dtype=jnp.int32), SIDE)
    first_core = lax.axis_index("core") == 0
    outer = jnp.where(first_core, y, x)
    inner = jnp.where(first_core, x, y)
    here = jnp.where(first_core, lax.axis_index("y"), lax.axis_index("x"))
    shift = (here - outer) % SIDE
    kv_order = outer * SIDE + inner
    q_order = jnp.where(shift == 2, 3, jnp.where(shift == 3, 2, shift)) * SIDE + inner

    far_rows = -(-(WINDOW - 1 - 2 * row_count) // 16) * 16
    kv, tail = projection(tokens, all_kv, kv_order, key_gain, tables, 1, far_rows)
    near = from_behind(kv, 1)
    far = from_behind(tail, 3)
    middle = from_behind(kv, 2)
    (queries,) = projection(tokens, all_q, q_order, query_gain, tables, 2)
    return attention(queries, [far, middle, near, kv], offset)


def solution(mesh):
    split = Mesh(mesh.devices.reshape(SIDE, SIDE, 2, 8, 2), CTX + HEAD)
    placed = (P(CTX, None), P(CTX, HEAD), P(CTX, HEAD), P(CTX, HEAD), P(), P())
    return jax.shard_map(
        on_device, mesh=split, in_specs=placed, out_specs=P(CTX, HEAD), check_vma=False
    )
```
